32 devices in a mesh: items: 8 (over y, x, core), seq: 4 (over z).
Axes of the slice: x: 2, y: 2, z: 4, core: 2. Of those that a mesh axis runs over, the one named last changes fastest.
Arguments:
- tokens: bfloat16 [24, 400, 768], P('items', 'seq'), may hold values from -6 to 6
- cotangent: bfloat16 [24, 400, 768], P('items', 'seq'), may hold values from -6 to 6
- ln1_gain: bfloat16 [768], replicated, may hold values from 0.099609375 to 1.8984375
- ln1_shift: bfloat16 [768], replicated, may hold values from -3 to 3
- w_query: bfloat16 [768, 768], replicated, may hold values from -0.21875 to 0.21875
- b_query: bfloat16 [768], replicated, may hold values from -3 to 3
- w_key: bfloat16 [768, 768], replicated, may hold values from -0.21875 to 0.21875
- w_value: bfloat16 [768, 768], replicated, may hold values from -0.21875 to 0.21875
- b_value: bfloat16 [768], replicated, may hold values from -3 to 3
- w_out: bfloat16 [768, 768], replicated, may hold values from -3.5 to 3.5
- b_out: bfloat16 [768], replicated, may hold values from -3 to 3
- ln2_gain: bfloat16 [768], replicated, may hold values from 0.099609375 to 1.8984375
- ln2_shift: bfloat16 [768], replicated, may hold values from -3 to 3
- w_inner: bfloat16 [768, 3072], replicated, may hold values from -0.21875 to 0.21875
- b_inner: bfloat16 [3072], replicated, may hold values from -3 to 3
- w_outer: bfloat16 [3072, 768], replicated, may hold values from -0.109375 to 0.109375
- b_outer: bfloat16 [768], replicated, may hold values from -3 to 3
- key_valid: int32 [24, 400], P('items'), may hold values from 0 to 1, as said below
Outputs:
- out_tokens: bfloat16 [24, 400, 768], P('items', 'seq')
- grad_tokens: bfloat16 [24, 400, 768], P('items', 'seq')
- grad_ln1_gain: float32 [768], replicated
- grad_ln1_shift: float32 [768], replicated
- grad_w_query: float32 [768, 768], replicated
- grad_b_query: float32 [768], replicated
- grad_w_key: float32 [768, 768], replicated
- grad_w_value: float32 [768, 768], replicated
- grad_b_value: float32 [768], replicated
- grad_w_out: float32 [768, 768], replicated
- grad_b_out: float32 [768], replicated
- grad_ln2_gain: float32 [768], replicated
- grad_ln2_shift: float32 [768], replicated
- grad_w_inner: float32 [768, 3072], replicated
- grad_b_inner: float32 [3072], replicated
- grad_w_outer: float32 [3072, 768], replicated
- grad_b_outer: float32 [768], replicated
The draws below stay inside these ranges and needn't reach their ends.
Inputs may be any that keep to these rules, and one draw needn't show every extreme that they name: `key_valid`: in each item the ones come first and the zeros last; an item has 1 to 3 zeros, and some item has exactly 3.
All inputs are finite; a program needn't handle non-finite values.
Results may differ from the reference program's by a relative error of at most 0.012.
The reference program's roundings to bfloat16 on the way count: a program that leaves them out, or rounds other values in their place, can miss the bound.
Values may be sent and summed in bfloat16 or wider, within the bound.
No kernel may reach another device: no remote copies, remote signals or barrier semaphores. Data moves between devices by JAX's collectives and lax.ppermute only.
A program may use at most 192 MiB of HBM per device.

```python
import jax
import jax.numpy as jnp
from jax import lax

D = 768
HEADS = 12
HEAD_DIM = 64
FF = 3072
ITEM_DEV = 3
SEQ = 400
PAD_MOST = 3
ITEMS = 24


def draw_key_valid(key, part):
    padding = jax.random.randint(key, (ITEMS,), 1, PAD_MOST + 1)
    padding = padding.at[0].set(PAD_MOST)
    limits = SEQ - padding
    position = jnp.arange(SEQ)
    return (position[None, :] < limits[:, None]).astype(jnp.int32)


def level_of(own_key, dims, shards, least, largest):
    def one(dim, parts):
        heights = jax.random.uniform(jax.random.fold_in(jax.random.fold_in(own_key, 6), dim), (parts,), jnp.float32, least / len(shards), largest / len(shards))
        return jnp.repeat(jnp.exp(heights), dims[dim] // parts).reshape((-1,) + (1,) * (len(dims) - dim - 1))

    loudness = one(*shards[0])
    for cut in shards[1:]:
        loudness = loudness * one(*cut)
    return loudness


def normal_values(rng, shape, width, limit, split=(), dtype=jnp.bfloat16):
    level = level_of(rng, shape, split, -0.22, 0.18) if split else 1.0
    values = jax.random.normal(rng, shape, jnp.float32) * width * level
    return jnp.minimum(jnp.maximum(values, -limit), limit).astype(dtype)


def setup_inputs(seed: int = 0) -> dict:
    seeds = jax.random.split(jax.random.key(seed), 19)
    tokens = normal_values(seeds[0], (ITEMS, SEQ, D), 1.0, 6.0, ((0, 8), (1, 4)))
    cotangent = normal_values(seeds[1], (ITEMS, SEQ, D), 1.0, 6.0, ((0, 8), (1, 4)))
    ln1_gain = jnp.clip(1.0 + 0.18 * jax.random.normal(seeds[2], (D,), jnp.float32), 0.099609375, 1.8984375).astype(jnp.bfloat16)
    ln1_shift = normal_values(seeds[3], (D,), 0.5, 3.0)
    w_query = normal_values(seeds[4], (D, D), D ** -0.5, 0.21875)
    b_query = normal_values(seeds[5], (D,), 0.5, 3.0)
    w_key = normal_values(seeds[6], (D, D), D ** -0.5, 0.21875)
    w_value = normal_values(seeds[7], (D, D), D ** -0.5, 0.21875)
    b_value = normal_values(seeds[8], (D,), 0.5, 3.0)
    w_out = normal_values(seeds[9], (D, D), (max(2 * D // SEQ, 1)) ** -0.5, 3.5)
    b_out = normal_values(seeds[10], (D,), 0.5, 3.0)
    ln2_gain = jnp.clip(1.0 + 0.18 * jax.random.normal(seeds[11], (D,), jnp.float32), 0.099609375, 1.8984375).astype(jnp.bfloat16)
    ln2_shift = normal_values(seeds[12], (D,), 0.5, 3.0)
    w_inner = normal_values(seeds[13], (D, FF), D ** -0.5, 0.21875)
    b_inner = normal_values(seeds[14], (FF,), 0.5, 3.0)
    w_outer = normal_values(seeds[15], (FF, D), FF ** -0.5, 0.109375)
    b_outer = normal_values(seeds[16], (D,), 0.5, 3.0)
    key_valid = draw_key_valid(jax.random.fold_in(seeds[18], 71), 0)
    return dict(tokens=tokens, cotangent=cotangent, ln1_gain=ln1_gain, ln1_shift=ln1_shift, w_query=w_query, b_query=b_query, w_key=w_key, w_value=w_value, b_value=b_value, w_out=w_out, b_out=b_out, ln2_gain=ln2_gain, ln2_shift=ln2_shift, w_inner=w_inner, b_inner=b_inner, w_outer=w_outer, b_outer=b_outer, key_valid=key_valid)


@jax.custom_vjp
def low(v):
    return lax.optimization_barrier(v.astype(jnp.bfloat16)).astype(jnp.float32)

@jax.custom_vjp
def low_back(v):
    return v

def low_keep(v):
    return (low(v), None)

def low_pass(kept, grad):
    return (grad,)

def back_keep(v):
    return (v, None)

def back_low(kept, grad):
    return (low(grad),)
low.defvjp(low_keep, low_pass)
low_back.defvjp(back_keep, back_low)
EPSILON = 1e-06
MASKED = -1000000000.0

def norm_rows(values, gain, shift):
    center = values - lax.optimization_barrier(jnp.mean(values, axis=-1, keepdims=True))
    spread = lax.optimization_barrier(jnp.mean(center * center, axis=-1, keepdims=True))
    return center * lax.rsqrt(spread + EPSILON) * gain + shift

def product(left, weight):
    return jnp.einsum('bti,ij->btj', left, weight, precision=lax.Precision.HIGHEST)

def forward(params, inputs, usable):
    ln1_gain, ln1_shift, w_query, b_query, w_key, w_value, b_value, w_out, b_out, ln2_gain, ln2_shift, w_inner, b_inner, w_outer, b_outer = params
    item_count, length, model_width = inputs.shape
    normed = low(norm_rows(inputs, ln1_gain, ln1_shift))
    query = low(low_back(product(normed, w_query) + b_query))
    keyset = low(low_back(product(normed, w_key)))
    values = low(low_back(product(normed, w_value) + b_value))
    shape_four = (item_count, length, HEADS, HEAD_DIM)
    scores = jnp.einsum('bqhd,bkhd->bhqk', query.reshape(shape_four), keyset.reshape(shape_four), precision=lax.Precision.HIGHEST) * HEAD_DIM ** (-0.5)
    scores = low_back(jnp.where(usable[:, None, None, :] > 0, scores, MASKED))
    row_top = lax.optimization_barrier(jnp.max(scores, axis=-1, keepdims=True))
    weights = jnp.exp(scores - row_top)
    probs = weights / lax.optimization_barrier(jnp.sum(weights, axis=-1, keepdims=True))
    mixed = jnp.einsum('bhqk,bkhd->bqhd', low(probs), values.reshape(shape_four), precision=lax.Precision.HIGHEST)
    mixed = low(low_back(mixed.reshape(item_count, length, model_width)))
    hidden = inputs + low_back(product(mixed, w_out)) + b_out
    normed_two = low(norm_rows(hidden, ln2_gain, ln2_shift))
    inner = low_back(product(normed_two, w_inner) + b_inner)
    active = low(jax.nn.gelu(inner, approximate=False))
    return hidden + low_back(product(active, w_outer)) + b_outer

def reference(tokens, cotangent, ln1_gain, ln1_shift, w_query, b_query, w_key, w_value, b_value, w_out, b_out, ln2_gain, ln2_shift, w_inner, b_inner, w_outer, b_outer, key_valid):
    params = tuple((item.astype(jnp.float32) for item in (ln1_gain, ln1_shift, w_query, b_query, w_key, w_value, b_value, w_out, b_out, ln2_gain, ln2_shift, w_inner, b_inner, w_outer, b_outer)))
    group_count = ITEMS // ITEM_DEV
    inputs = tokens.astype(jnp.float32).reshape(group_count, ITEM_DEV, SEQ, D)
    cotangents = cotangent.astype(jnp.float32).reshape(group_count, ITEM_DEV, SEQ, D)
    usable = key_valid.reshape(group_count, ITEM_DEV, SEQ)

    def advance(totals, pieces):
        block_in, block_cot, block_valid = pieces
        result, pullback = jax.vjp(lambda weights, block: forward(weights, block, block_valid), params, block_in)
        grad_params, grad_block = pullback(block_cot)
        totals = jax.tree.map(lambda first, second: first + second, totals, grad_params)
        return (totals, (result.astype(jnp.bfloat16), grad_block.astype(jnp.bfloat16)))
    zeroed = tuple((jnp.zeros_like(item) for item in params))
    grads, (results, grad_blocks) = lax.scan(advance, zeroed, (inputs, cotangents, usable))
    out_tokens = results.reshape(ITEMS, SEQ, D)
    grad_tokens = grad_blocks.reshape(ITEMS, SEQ, D)
    g_ln1_gain, g_ln1_shift, g_w_query, g_b_query, g_w_key, g_w_value, g_b_value, g_w_out, g_b_out, g_ln2_gain, g_ln2_shift, g_w_inner, g_b_inner, g_w_outer, g_b_outer = grads
    return (out_tokens, grad_tokens, g_ln1_gain, g_ln1_shift, g_w_query, g_b_query, g_w_key, g_w_value, g_b_value, g_w_out, g_b_out, g_ln2_gain, g_ln2_shift, g_w_inner, g_b_inner, g_w_outer, g_b_outer)
```

```python
import jax
import jax.numpy as jnp
from jax import lax
from jax.sharding import PartitionSpec as P

D = 768
HEADS = 12
HEAD_DIM = 64
FF = 3072


EPSILON = 1e-06
MASKED = -1000000000.0
F32 = jnp.float32
BF16 = jnp.bfloat16


def norm_parts(values):
    center = values - jnp.mean(values, axis=-1, keepdims=True)
    spread = jnp.mean(center * center, axis=-1, keepdims=True)
    scale = lax.rsqrt(spread + EPSILON)
    return center * scale, scale


def norm_back(unit, scale, grads):
    drop = jnp.mean(grads, axis=-1, keepdims=True)
    turn = jnp.mean(grads * unit, axis=-1, keepdims=True)
    return scale * (grads - drop - unit * turn)


def dot(left, right, dims):
    return lax.dot_general(left, right, (dims, ((), ())), preferred_element_type=F32)


def tall_dot(left, right):
    return dot(left, right, ((0,), (0,)))


def wide_dot(left, weight):
    return dot(left, weight, ((1,), (0,)))


def back_dot(grads, weight):
    return dot(grads, weight, ((1,), (1,)))


def column_sum(values):
    return jnp.sum(values.astype(F32), axis=0)


def take_item(values, mask_idle):
    groups = lax.axis_size("seq")
    here = lax.axis_index("seq")
    count = values.shape[0]
    blocks = []
    for step in range(groups):
        pick = jnp.minimum(lax.rem(here + step, groups), count - 1)
        block = lax.dynamic_index_in_dim(values, pick, 0, keepdims=False)
        if step == 0:
            if mask_idle:
                block = jnp.where(here < count, block, jnp.zeros_like(block))
        else:
            pairs = [(s, (s + step) % groups) for s in range(groups) if (s + step) % groups < count]
            block = lax.ppermute(block, "seq", pairs)
        blocks.append(block)
    return jnp.concatenate(blocks, axis=0)


def give_item(values, count):
    groups = lax.axis_size("seq")
    here = lax.axis_index("seq")
    blocks = values.reshape(groups, -1, values.shape[-1])
    got = []
    for step in range(groups):
        block = blocks[step]
        if step:
            block = lax.ppermute(block, "seq", [(s, (s - step) % groups) for s in range(count)])
        got.append(block)
    ring = jnp.stack(got + got)
    return lax.dynamic_slice_in_dim(ring, lax.rem(groups - here, groups), count, 0)


def item_mask(valid):
    groups = lax.axis_size("seq")
    here = lax.axis_index("seq")
    row = lax.dynamic_index_in_dim(valid, jnp.minimum(here, valid.shape[0] - 1), 0, keepdims=False)
    row = row.reshape(groups, -1)
    order = lax.rem(here + groups - jnp.arange(groups), groups)
    chosen = order[:, None] == jnp.arange(groups)[None, :]
    return jnp.sum(jnp.where(chosen[:, :, None], row[None], 0), axis=1).reshape(-1)


def swap(values, axis, bit):
    size = lax.axis_size(axis)
    return lax.ppermute(values, axis, [(i, i ^ (1 << bit)) for i in range(size)])


def bit_of(axis, bit):
    return lax.rem(lax.div(lax.axis_index(axis), 1 << bit), 2)


def add_low(first, second):
    return (first.astype(F32) + second.astype(F32)).astype(BF16)


def halve(values, axis, bit):
    half = values.shape[0] // 2
    side = bit_of(axis, bit)
    keep = lax.dynamic_slice_in_dim(values, side * half, half, 0)
    send = lax.dynamic_slice_in_dim(values, (1 - side) * half, half, 0)
    return add_low(keep, swap(send, axis, bit))


def double(values, axis, bit):
    other = swap(values, axis, bit)
    upper = bit_of(axis, bit) > 0
    return jnp.concatenate(
        [jnp.where(upper, other, values), jnp.where(upper, values, other)], axis=0
    )


def bits_of(axis):
    return lax.axis_size(axis).bit_length() - 1


def sum_rows(values):
    dims = [("items", b) for b in range(1, bits_of("items"))] + [("seq", 0)]
    last = [("seq", b) for b in range(1, bits_of("seq"))]
    mine = halve(values, "items", 0)
    count = mine.shape[0] // 3
    parts = [mine[i * count : (i + 1) * count] for i in range(3)]
    orders = [dims[i % len(dims) :] + dims[: i % len(dims)] for i in range(3)]
    for step in range(len(dims)):
        parts = [halve(p, *o[step]) for p, o in zip(parts, orders)]
    if last:
        size = parts[0].shape[0]
        joined = jnp.concatenate(parts, axis=0)
        for axis, bit in last:
            joined = add_low(joined, swap(joined, axis, bit))
        parts = [joined[i * size : (i + 1) * size] for i in range(3)]
    for step in reversed(range(len(dims))):
        parts = [double(p, *o[step]) for p, o in zip(parts, orders)]
    return double(jnp.concatenate(parts, axis=0), "items", 0)


def sum_small(values):
    for axis in ("items", "seq"):
        for bit in range(bits_of(axis)):
            values = values + swap(values, axis, bit)
    return values


def attend_scores(query, keyset, usable):
    scores = jnp.einsum("qhd,khd->hqk", query, keyset, preferred_element_type=F32)
    return jnp.where(usable[None, None, :] > 0, scores * HEAD_DIM ** (-0.5), MASKED)


def local(
    tokens,
    cotangent,
    ln1_gain,
    ln1_shift,
    w_query,
    b_query,
    w_key,
    w_value,
    b_value,
    w_out,
    b_out,
    ln2_gain,
    ln2_shift,
    w_inner,
    b_inner,
    w_outer,
    b_outer,
    key_valid,
):
    count = tokens.shape[0]
    factor = HEAD_DIM ** (-0.5)
    rows = take_item(tokens, False)
    cot = take_item(cotangent, True)
    usable = item_mask(key_valid)
    length = rows.shape[0]
    four = (length, HEADS, HEAD_DIM)
    inputs = rows.astype(F32)
    unit1, scale1 = norm_parts(inputs)
    normed = (unit1 * ln1_gain.astype(F32) + ln1_shift.astype(F32)).astype(BF16)
    query = (wide_dot(normed, w_query) + b_query.astype(F32)).astype(BF16).reshape(four)
    keyset = wide_dot(normed, w_key).astype(BF16).reshape(four)
    values = (wide_dot(normed, w_value) + b_value.astype(F32)).astype(BF16).reshape(four)
    scores = attend_scores(query, keyset, usable)
    row_top = jnp.max(scores, axis=-1, keepdims=True)
    weights = jnp.exp(scores - row_top)
    probs = weights / jnp.sum(weights, axis=-1, keepdims=True)
    probs_low = probs.astype(BF16)
    mixed = jnp.einsum("hqk,khd->qhd", probs_low, values, preferred_element_type=F32)
    mixed = mixed.astype(BF16).reshape(length, D)
    hidden = inputs + wide_dot(mixed, w_out) + b_out.astype(F32)
    unit2, scale2 = norm_parts(hidden)
    normed2 = (unit2 * ln2_gain.astype(F32) + ln2_shift.astype(F32)).astype(BF16)
    inner = wide_dot(normed2, w_inner) + b_inner.astype(F32)
    phi = 0.5 * (1.0 + lax.erf(inner * (0.5**0.5)))
    active = (inner * phi).astype(BF16)
    slope = phi + inner * jnp.exp(-0.5 * inner * inner) * 0.3989422804014327
    result = hidden + wide_dot(active, w_outer) + b_outer.astype(F32)
    out_tokens = give_item(result.astype(BF16), count)
    g_outer = tall_dot(active, cot).astype(BF16)
    g_b_outer = column_sum(cot)
    d_inner_f = back_dot(cot, w_outer) * slope
    d_inner = d_inner_f.astype(BF16)
    g_inner = [
        tall_dot(normed2, d_inner[:, i * D : (i + 1) * D]).astype(BF16) for i in range(FF // D)
    ]
    g_b_inner = column_sum(d_inner)
    sum_ffn = sum_rows(jnp.concatenate([g_outer] + g_inner, axis=0))
    d_normed2 = back_dot(d_inner, w_inner)
    g_gain2 = column_sum(d_normed2 * unit2)
    g_shift2 = column_sum(d_normed2)
    d_hidden = cot.astype(F32) + norm_back(unit2, scale2, d_normed2 * ln2_gain.astype(F32))
    g_b_out = column_sum(d_hidden)
    d_hidden_low = d_hidden.astype(BF16)
    g_out = tall_dot(mixed, d_hidden_low).astype(BF16)
    d_mixed = back_dot(d_hidden_low, w_out).astype(BF16).reshape(four)
    d_value = jnp.einsum("hqk,qhd->khd", probs_low, d_mixed, preferred_element_type=F32)
    d_probs = jnp.einsum("qhd,khd->hqk", d_mixed, values, preferred_element_type=F32)
    weighted = jnp.sum(probs * d_probs, axis=-1, keepdims=True)
    d_scores = (probs * (d_probs - weighted)).astype(BF16)
    d_query = jnp.einsum("hqk,khd->qhd", d_scores, keyset, preferred_element_type=F32) * factor
    d_key = jnp.einsum("hqk,qhd->khd", d_scores, query, preferred_element_type=F32) * factor
    d_query = d_query.astype(BF16).reshape(length, D)
    d_key = d_key.astype(BF16).reshape(length, D)
    d_value = d_value.astype(BF16).reshape(length, D)
    g_attn = [tall_dot(normed, d).astype(BF16) for d in (d_query, d_key, d_value)]
    sum_attn = sum_rows(jnp.concatenate(g_attn + [g_out], axis=0))
    g_b_query = column_sum(d_query)
    g_b_value = column_sum(d_value)
    d_normed = back_dot(d_query, w_query) + back_dot(d_key, w_key) + back_dot(d_value, w_value)
    g_gain1 = column_sum(d_normed * unit1)
    g_shift1 = column_sum(d_normed)
    d_rows = d_hidden + norm_back(unit1, scale1, d_normed * ln1_gain.astype(F32))
    grad_tokens = give_item(d_rows.astype(BF16), count)
    small = [g_gain1, g_shift1, g_b_query, g_b_value, g_b_out, g_gain2, g_shift2, g_b_outer]
    small = jnp.stack(small + [g_b_inner[i * D : (i + 1) * D] for i in range(FF // D)])
    small = sum_small(small)
    sum_ffn = sum_ffn.astype(F32)
    sum_attn = sum_attn.astype(F32)
    sum_outer = sum_ffn[:FF]
    sum_inner = jnp.concatenate([sum_ffn[FF + i * D : FF + (i + 1) * D] for i in range(FF // D)], 1)
    sum_query, sum_key, sum_value, sum_out = (sum_attn[i * D : (i + 1) * D] for i in range(4))
    return (
        out_tokens,
        grad_tokens,
        small[0],
        small[1],
        sum_query,
        small[2],
        sum_key,
        sum_value,
        small[3],
        sum_out,
        small[4],
        small[5],
        small[6],
        sum_inner,
        small[8:].reshape(-1),
        sum_outer,
        small[7],
    )


def solution(mesh):
    by_rows = P("items", "seq", None)
    in_specs = (by_rows, by_rows) + (P(),) * 15 + (P("items", None),)
    out_specs = (by_rows, by_rows) + (P(),) * 15
    return jax.shard_map(local, mesh=mesh, in_specs=in_specs, out_specs=out_specs, check_vma=False)
```

```python
import jax
import jax.numpy as jnp
from jax import lax
from jax.sharding import PartitionSpec as P

D = 768
HEADS = 12
HEAD_DIM = 64
FF = 3072


EPSILON = 1e-06
MASKED = -1000000000.0
F32 = jnp.float32
BF16 = jnp.bfloat16


def norm_parts(values):
    center = values - jnp.mean(values, axis=-1, keepdims=True)
    spread = jnp.mean(center * center, axis=-1, keepdims=True)
    scale = lax.rsqrt(spread + EPSILON)
    return center * scale, scale


def norm_back(unit, scale, grads):
    drop = jnp.mean(grads, axis=-1, keepdims=True)
    turn = jnp.mean(grads * unit, axis=-1, keepdims=True)
    return scale * (grads - drop - unit * turn)


def dot(left, right, dims):
    return lax.dot_general(left, right, (dims, ((), ())), preferred_element_type=F32)


def tall_dot(left, right):
    return dot(left, right, ((0,), (0,)))


def wide_dot(left, weight):
    return dot(left, weight, ((1,), (0,)))


def back_dot(grads, weight):
    return dot(grads, weight, ((1,), (1,)))


def column_sum(values):
    return jnp.sum(values.astype(F32), axis=0)


def take_item(values, mask_idle):
    groups = lax.axis_size("seq")
    here = lax.axis_index("seq")
    count = values.shape[0]
    blocks = []
    for step in range(groups):
        pick = jnp.minimum(lax.rem(here + step, groups), count - 1)
        block = lax.dynamic_index_in_dim(values, pick, 0, keepdims=False)
        if step == 0:
            if mask_idle:
                block = jnp.where(here < count, block, jnp.zeros_like(block))
        else:
            pairs = [(s, (s + step) % groups) for s in range(groups) if (s + step) % groups < count]
            block = lax.ppermute(block, "seq", pairs)
        blocks.append(block)
    return jnp.concatenate(blocks, axis=0)


def give_item(values, count):
    groups = lax.axis_size("seq")
    here = lax.axis_index("seq")
    blocks = values.reshape(groups, -1, values.shape[-1])
    got = []
    for step in range(groups):
        block = blocks[step]
        if step:
            block = lax.ppermute(block, "seq", [(s, (s - step) % groups) for s in range(count)])
        got.append(block)
    ring = jnp.stack(got + got)
    return lax.dynamic_slice_in_dim(ring, lax.rem(groups - here, groups), count, 0)


def item_mask(valid):
    groups = lax.axis_size("seq")
    here = lax.axis_index("seq")
    row = lax.dynamic_index_in_dim(valid, jnp.minimum(here, valid.shape[0] - 1), 0, keepdims=False)
    row = row.reshape(groups, -1)
    order = lax.rem(here + groups - jnp.arange(groups), groups)
    chosen = order[:, None] == jnp.arange(groups)[None, :]
    return jnp.sum(jnp.where(chosen[:, :, None], row[None], 0), axis=1).reshape(-1)


def swap(values, axis, bit):
    size = lax.axis_size(axis)
    return lax.ppermute(values, axis, [(i, i ^ (1 << bit)) for i in range(size)])


def bit_of(axis, bit):
    return lax.rem(lax.div(lax.axis_index(axis), 1 << bit), 2)


def add_low(first, second):
    return (first.astype(F32) + second.astype(F32)).astype(BF16)


def halve(values, axis, bit):
    half = values.shape[0] // 2
    side = bit_of(axis, bit)
    keep = lax.dynamic_slice_in_dim(values, side * half, half, 0)
    send = lax.dynamic_slice_in_dim(values, (1 - side) * half, half, 0)
    return add_low(keep, swap(send, axis, bit))


def double(values, axis, bit):
    other = swap(values, axis, bit)
    upper = bit_of(axis, bit) > 0
    return jnp.concatenate(
        [jnp.where(upper, other, values), jnp.where(upper, values, other)], axis=0
    )


def bits_of(axis):
    return lax.axis_size(axis).bit_length() - 1


def level_orders():
    dims = [("items", b) for b in range(1, bits_of("items"))] + [("seq", 0)]
    return [dims[i % len(dims) :] + dims[: i % len(dims)] for i in range(3)]


def split_rows(values):
    count = values.shape[0] // 3
    return [values[i * count : (i + 1) * count] for i in range(3)]


def down_level(parts, step):
    return [halve(p, *o[step]) for p, o in zip(parts, level_orders())]


def finish_rows(parts, step):
    orders = level_orders()
    last = [("seq", b) for b in range(1, bits_of("seq"))]
    for level in range(step, len(orders[0])):
        parts = down_level(parts, level)
    if last:
        joined = jnp.concatenate(parts, axis=0)
        for axis, bit in last:
            joined = add_low(joined, swap(joined, axis, bit))
        parts = split_rows(joined)
    for level in reversed(range(len(orders[0]))):
        parts = [double(p, *o[level]) for p, o in zip(parts, orders)]
    mine = jnp.concatenate(parts, axis=0)
    other = swap(mine, "items", 0)
    upper = bit_of("items", 0) > 0

    def lower_rows(first, stop):
        return jnp.where(upper, other[first:stop], mine[first:stop]).astype(F32)

    def upper_rows(first, stop):
        return jnp.where(upper, mine[first:stop], other[first:stop]).astype(F32)

    return lower_rows, upper_rows


def tie(parts, value):
    tied = lax.optimization_barrier(tuple(parts) + (value,))
    return list(tied[:-1]), tied[-1]


def sum_small(values):
    for axis in ("items", "seq"):
        for bit in range(bits_of(axis)):
            values = values + swap(values, axis, bit)
    return values


def attend_scores(query, keyset, usable):
    scores = jnp.einsum("qhd,khd->hqk", query, keyset, preferred_element_type=F32)
    return jnp.where(usable[None, None, :] > 0, scores * HEAD_DIM ** (-0.5), MASKED)


def local(
    tokens,
    cotangent,
    ln1_gain,
    ln1_shift,
    w_query,
    b_query,
    w_key,
    w_value,
    b_value,
    w_out,
    b_out,
    ln2_gain,
    ln2_shift,
    w_inner,
    b_inner,
    w_outer,
    b_outer,
    key_valid,
):
    count = tokens.shape[0]
    factor = HEAD_DIM ** (-0.5)
    rows = take_item(tokens, False)
    cot = take_item(cotangent, True)
    usable = item_mask(key_valid)
    length = rows.shape[0]
    four = (length, HEADS, HEAD_DIM)
    inputs = rows.astype(F32)
    unit1, scale1 = norm_parts(inputs)
    normed = (unit1 * ln1_gain.astype(F32) + ln1_shift.astype(F32)).astype(BF16)
    query = (wide_dot(normed, w_query) + b_query.astype(F32)).astype(BF16).reshape(four)
    keyset = wide_dot(normed, w_key).astype(BF16).reshape(four)
    values = (wide_dot(normed, w_value) + b_value.astype(F32)).astype(BF16).reshape(four)
    scores = attend_scores(query, keyset, usable)
    row_top = jnp.max(scores, axis=-1, keepdims=True)
    weights = jnp.exp(scores - row_top)
    probs = weights / jnp.sum(weights, axis=-1, keepdims=True)
    probs_low = probs.astype(BF16)
    mixed = jnp.einsum("hqk,khd->qhd", probs_low, values, preferred_element_type=F32)
    mixed = mixed.astype(BF16).reshape(length, D)
    hidden = inputs + wide_dot(mixed, w_out) + b_out.astype(F32)
    unit2, scale2 = norm_parts(hidden)
    normed2 = (unit2 * ln2_gain.astype(F32) + ln2_shift.astype(F32)).astype(BF16)
    inner = wide_dot(normed2, w_inner) + b_inner.astype(F32)
    phi = 0.5 * (1.0 + lax.erf(inner * (0.5**0.5)))
    active = (inner * phi).astype(BF16)
    slope = phi + inner * jnp.exp(-0.5 * inner * inner) * 0.3989422804014327
    result = hidden + wide_dot(active, w_outer) + b_outer.astype(F32)
    out_tokens = give_item(result.astype(BF16), count)
    g_outer = tall_dot(active, cot).astype(BF16)
    g_b_outer = column_sum(cot)
    d_inner_f = back_dot(cot, w_outer) * slope
    d_inner = d_inner_f.astype(BF16)
    g_inner = [
        tall_dot(normed2, d_inner[:, i * D : (i + 1) * D]).astype(BF16) for i in range(FF // D)
    ]
    g_b_inner = column_sum(d_inner)
    ffn = jnp.concatenate([g_outer] + g_inner, axis=0)
    (ffn,), d_inner = tie([ffn], d_inner)
    mine = halve(ffn, "items", 0)
    d_normed2 = back_dot(d_inner, w_inner)
    g_gain2 = column_sum(d_normed2 * unit2)
    g_shift2 = column_sum(d_normed2)
    d_hidden = cot.astype(F32) + norm_back(unit2, scale2, d_normed2 * ln2_gain.astype(F32))
    g_b_out = column_sum(d_hidden)
    d_hidden_low = d_hidden.astype(BF16)
    (mine,), d_hidden_low = tie([mine], d_hidden_low)
    parts = down_level(split_rows(mine), 0)
    g_out = tall_dot(mixed, d_hidden_low).astype(BF16)
    d_mixed = back_dot(d_hidden_low, w_out).astype(BF16).reshape(four)
    d_value = jnp.einsum("hqk,qhd->khd", probs_low, d_mixed, preferred_element_type=F32)
    d_probs = jnp.einsum("qhd,khd->hqk", d_mixed, values, preferred_element_type=F32)
    weighted = jnp.sum(probs * d_probs, axis=-1, keepdims=True)
    parts, weighted = tie(parts, weighted)
    parts = down_level(parts, 1)
    d_scores = (probs * (d_probs - weighted)).astype(BF16)
    parts, d_scores = tie(parts, d_scores)
    ffn_lower, ffn_upper = finish_rows(parts, 2)
    d_query = jnp.einsum("hqk,khd->qhd", d_scores, keyset, preferred_element_type=F32) * factor
    d_key = jnp.einsum("hqk,qhd->khd", d_scores, query, preferred_element_type=F32) * factor
    d_query = d_query.astype(BF16).reshape(length, D)
    d_key = d_key.astype(BF16).reshape(length, D)
    d_value = d_value.astype(BF16).reshape(length, D)
    g_attn = [tall_dot(normed, d).astype(BF16) for d in (d_query, d_key, d_value)]
    mine = halve(jnp.concatenate(g_attn + [g_out], axis=0), "items", 0)
    attn_lower, attn_upper = finish_rows(split_rows(mine), 0)
    g_b_query = column_sum(d_query)
    g_b_value = column_sum(d_value)
    d_normed = back_dot(d_query, w_query) + back_dot(d_key, w_key) + back_dot(d_value, w_value)
    g_gain1 = column_sum(d_normed * unit1)
    g_shift1 = column_sum(d_normed)
    d_rows = d_hidden + norm_back(unit1, scale1, d_normed * ln1_gain.astype(F32))
    grad_tokens = give_item(d_rows.astype(BF16), count)
    small = [g_gain1, g_shift1, g_b_query, g_b_value, g_b_out, g_gain2, g_shift2, g_b_outer]
    small = jnp.stack(small + [g_b_inner[i * D : (i + 1) * D] for i in range(FF // D)])
    small = sum_small(small)
    sum_outer = ffn_lower(0, FF)
    sum_inner = jnp.concatenate([ffn_upper(i * D, (i + 1) * D) for i in range(FF // D)], 1)
    sum_query, sum_key = attn_lower(0, D), attn_lower(D, 2 * D)
    sum_value, sum_out = attn_upper(0, D), attn_upper(D, 2 * D)
    return (
        out_tokens,
        grad_tokens,
        small[0],
        small[1],
        sum_query,
        small[2],
        sum_key,
        sum_value,
        small[3],
        sum_out,
        small[4],
        small[5],
        small[6],
        sum_inner,
        small[8:].reshape(-1),
        sum_outer,
        small[7],
    )


def solution(mesh):
    by_rows = P("items", "seq", None)
    in_specs = (by_rows, by_rows) + (P(),) * 15 + (P("items", None),)
    out_specs = (by_rows, by_rows) + (P(),) * 15
    return jax.shard_map(local, mesh=mesh, in_specs=in_specs, out_specs=out_specs, check_vma=False)
```
